256 devices in a mesh: tm: 32 (over z, x_hi, core), chan: 8 (over x_lo, y).
Axes of the slice: x: 4 (x_hi: 2, x_lo: 2; x = x_hi * 2 + x_lo), y: 4, z: 8, core: 2. Of those that a mesh axis runs over, the one named last changes fastest.
Arguments:
- raw_traces: bfloat16 [5120, 131072], P('chan', 'tm'), may hold values from -120 to 120
- fir_taps: bfloat16 [128], replicated, may hold values from -0.5 to 0.5
- sources: int32 [512], replicated, may hold values from 0 to 5119, as said below
- dead_flags: int32 [5120], P('chan'), may hold values 0 or 1
Outputs:
- correlations: float32 [512, 8, 5120], P('tm', None, 'chan')
The draws below stay inside these ranges and needn't reach their ends.
Inputs may be any that keep to these rules, and one draw needn't show every extreme that they name: `sources`: 512 distinct channel indices; no group of 640 channels that share c // 640 holds more than 128 of them, and one group holds exactly 128.
All inputs are finite; a program needn't handle non-finite values. No bound on the sum of `dead_flags` on one device may be relied on, other than what follows from the above.
Results may differ from the reference program's by a relative error of at most 0.013.
Values may be sent and summed in bfloat16 or wider, within the bound.
A program may use at most 64 MiB of HBM per device.

```python
import math
import jax
import jax.numpy as jnp
from jax import lax

CH_DEV = 640
VS = 512
TD = 256
NWIN = 4
NLAG = 8
HW = 32
TAPS = 128
DECIM = 4
CH = 5120
WINDOWS = 128
TRAW = 131072
MOST = 128
N_CHAN = 8


def draw_raw_traces(key, part):
    key_noise, key_chan, key_block = jax.random.split(key, 3)
    chan_scale = jnp.exp(jax.random.uniform(key_chan, (CH, 1, 1), jnp.float32, 0.0, math.log(10.0)))
    block_scale = jnp.exp(jax.random.uniform(key_block, (CH, TRAW // 512, 1), jnp.float32, 0.0, math.log(3.0)))
    noise = jnp.clip(jax.random.normal(key_noise, (CH, TRAW), jnp.float32), -4.0, 4.0)
    scaled = noise.reshape(CH, TRAW // 512, 512) * block_scale * chan_scale
    return scaled.reshape(CH, TRAW).astype(jnp.bfloat16)


def draw_sources(key, part):
    key_groups, key_chans, key_order = jax.random.split(key, 3)
    slot_ids = jnp.arange(VS)
    others = N_CHAN - 1
    remain = jnp.maximum(slot_ids - MOST, 0)
    layout = jnp.where(slot_ids < MOST, 0, 1 + remain % others)
    slot_rank = jnp.where(slot_ids < MOST, slot_ids, remain // others)
    group_perm = jax.random.permutation(key_groups, N_CHAN)
    group = group_perm[layout]
    chan_keys = jax.random.split(key_chans, N_CHAN)
    chan_perm = jax.vmap(lambda one_key: jax.random.permutation(one_key, CH_DEV))(chan_keys)
    channel = group * CH_DEV + chan_perm[group, slot_rank]
    order = jax.random.permutation(key_order, VS)
    return channel[order].astype(jnp.int32)


def touch_ends(values, stream_key, low, top_value):
    longest = values.shape.index(max(values.shape))
    spots = []
    for shift in (0, 1):
        where = [jax.random.randint(jax.random.fold_in(stream_key, axis), (), 0, length) for axis, length in enumerate(values.shape)]
        where[longest] = (where[longest] + shift) % values.shape[longest]
        spots.append(tuple(where))
    return values.at[spots[0]].set(low).at[spots[1]].set(top_value)


def normal_values(own_key, dims, spread, bound, kind=jnp.bfloat16):
    result = spread * jax.random.normal(own_key, dims, jnp.float32)
    return jnp.clip(result, min=-bound, max=bound).astype(kind)


def setup_inputs(seed: int = 0) -> dict:
    keys = jax.random.split(jax.random.key(seed), 5)
    raw_traces = draw_raw_traces(jax.random.fold_in(keys[4], 71), 0)
    fir_taps = normal_values(keys[1], (TAPS,), 0.1, 0.5)
    sources = draw_sources(jax.random.fold_in(keys[4], 71), 0)
    dead_flags = touch_ends((jax.random.randint(keys[3], (CH,), 0, 8) < 1).astype(jnp.int32), jax.random.fold_in(keys[3], 1), 0, 1)
    return dict(raw_traces=raw_traces, fir_taps=fir_taps, sources=sources, dead_flags=dead_flags)


def fir_rows(fir_taps, out_block):
    width = TAPS + DECIM * out_block
    padded_taps = jnp.concatenate([jnp.zeros((1,), jnp.bfloat16), fir_taps, jnp.zeros((width + DECIM - TAPS - 1,), jnp.bfloat16)])
    return jnp.tile(padded_taps, out_block)[:out_block * width].reshape(out_block, width)

def dft_table():
    time_index = jnp.arange(TD)[:, None]
    freq_index = jnp.arange(TD // 2)[None, :]
    phase = time_index * freq_index % TD
    angles = 2.0 * math.pi / TD * phase.astype(jnp.float32)
    return jnp.concatenate([jnp.cos(angles), -jnp.sin(angles)], axis=1).astype(jnp.bfloat16)

def lag_tables():
    lag_shift = jnp.arange(NLAG) - NLAG // 2
    freq_index = jnp.arange(TD // 2)
    phase = lag_shift[:, None] * freq_index[None, :] % TD
    angles = 2.0 * math.pi / TD * phase.astype(jnp.float32)
    return (jnp.cos(angles), jnp.sin(angles))

def band_matrix():
    bin_index = jnp.arange(TD // 2)
    return (jnp.abs(bin_index[:, None] - bin_index[None, :]) <= HW).astype(jnp.float32)

def whiten(spectrum, alive):
    half_bins = TD // 2
    real_part = spectrum[..., :half_bins]
    imag_part = spectrum[..., half_bins:]
    amplitude = jnp.sqrt(real_part * real_part + imag_part * imag_part)
    mean_level = jnp.einsum('cwf,fg->cwg', amplitude, band_matrix(), precision=lax.Precision.HIGHEST) / (2 * HW + 1)
    factor = alive / (mean_level + 1e-06)
    return (spectrum * jnp.concatenate([factor, factor], axis=-1)).astype(jnp.bfloat16)

def rotate(source, gain_scale):
    half_bins = TD // 2
    real_src = source[..., :half_bins].astype(jnp.float32)[:, None]
    imag_src = source[..., half_bins:].astype(jnp.float32)[:, None]
    cos_lag, sin_lag = lag_tables()
    cos_lag = cos_lag[None, :, None, :]
    sin_lag = sin_lag[None, :, None, :]
    real_out = (real_src * cos_lag + imag_src * sin_lag) * gain_scale
    imag_out = (imag_src * cos_lag - real_src * sin_lag) * gain_scale
    return jnp.concatenate([real_out, imag_out], axis=-1).astype(jnp.bfloat16)

def decimate(raw_block, fir_taps):
    out_block = min(128, NWIN * TD)
    sample_block = DECIM * out_block
    row_count = raw_block.shape[0]
    grouped = raw_block.reshape(row_count, -1, sample_block)
    before = jnp.concatenate([jnp.zeros((row_count, 1, TAPS), jnp.bfloat16), grouped[:, :-1, sample_block - TAPS:]], axis=1)
    window = jnp.concatenate([before, grouped], axis=2).reshape(-1, TAPS + sample_block)
    matrix = fir_rows(fir_taps, out_block)
    dec = jnp.dot(window.astype(jnp.float32), matrix.T.astype(jnp.float32), preferred_element_type=jnp.float32)
    return dec.astype(jnp.bfloat16).reshape(row_count, -1)

def spectra(raw_block, dead_block, fir_taps):
    dec = decimate(raw_block, fir_taps)
    row_count = dec.shape[0]
    spectrum = jnp.dot(dec.reshape(-1, TD).astype(jnp.float32), dft_table().astype(jnp.float32), preferred_element_type=jnp.float32)
    spectrum = spectrum.reshape(row_count, -1, TD)
    alive = (1 - dead_block).astype(jnp.float32)[:, None, None]
    return whiten(spectrum, alive)

def reference(raw_traces, fir_taps, sources, dead_flags):
    block_count = CH // CH_DEV

    def prepare(segment):
        raw_block, dead_block = segment
        return spectra(raw_block, dead_block, fir_taps)
    whitened = lax.map(prepare, (raw_traces.reshape(block_count, CH_DEV, TRAW), dead_flags.reshape(block_count, CH_DEV)))
    whitened = whitened.reshape(CH, WINDOWS, TD)
    source = jnp.take(whitened, sources, axis=0)
    gain_scale = 1.0 / math.sqrt(WINDOWS * TD)
    seg_count = WINDOWS // NWIN
    white_seg = whitened.reshape(CH, seg_count, NWIN * TD).transpose(1, 0, 2)
    source_seg = source.reshape(VS, seg_count, NWIN, TD).transpose(1, 0, 2, 3)

    def add_segment(stacked, segment):
        src_part, white_part = segment
        lagged = rotate(src_part, gain_scale).reshape(VS * NLAG, NWIN * TD)
        partial_value = jnp.dot(lagged.astype(jnp.float32), white_part.T.astype(jnp.float32), preferred_element_type=jnp.float32)
        rounded = lax.optimization_barrier(partial_value.astype(jnp.bfloat16))
        return (stacked + rounded.astype(jnp.float32), None)
    stacked, unused = lax.scan(add_segment, jnp.zeros((VS * NLAG, CH), jnp.float32), (source_seg, white_seg))
    return stacked.reshape(VS, NLAG, CH)
```

```python
import functools
import math

import jax
import jax.numpy as jnp
import numpy as np
from jax import lax
from jax.experimental import pallas as pl
from jax.experimental.pallas import tpu as pltpu
from jax.sharding import PartitionSpec as P

VS = 512
TD = 256
NWIN = 4
NLAG = 8
HW = 32
TAPS = 128
DECIM = 4
HALF = TD // 2
MESH = pl.DeviceIdType.MESH
F32 = jnp.float32
BF16 = jnp.bfloat16
NT = (((1,), (1,)), ((), ()))

ZN = 8
GN = 8
SUBS = 2
LEAD_AG = 2
LEAD_RS = 4


def fir_rows(fir_taps, out_block):
    width = TAPS + DECIM * out_block
    padded_taps = jnp.concatenate(
        [jnp.zeros((1,), BF16), fir_taps, jnp.zeros((width + DECIM - TAPS - 1,), BF16)]
    )
    return jnp.tile(padded_taps, out_block)[: out_block * width].reshape(out_block, width)


def dft_table():
    phase = np.arange(TD)[:, None] * np.arange(HALF)[None, :] % TD
    angles = np.float32(2.0 * math.pi / TD) * phase.astype(np.float32)
    return jnp.asarray(np.concatenate([np.cos(angles), -np.sin(angles)], axis=1), dtype=BF16)


def lag_tables(gain):
    phase = np.arange(NLAG)[:, None] * np.arange(HALF)[None, :] % TD
    angles = np.float32(2.0 * math.pi / TD) * phase.astype(np.float32)
    both = np.concatenate([np.cos(angles), np.sin(angles)], axis=1)
    return jnp.asarray((both * np.float32(gain)).astype(np.float32))


def band_matrix():
    bins = np.arange(HALF)
    return jnp.asarray(np.abs(bins[:, None] - bins[None, :]) <= HW, dtype=BF16)


def kernel(
    raw_ref, fir_ref, table_ref, band_ref, lag_ref, src_ref, dead_ref, out_ref,
    raw, w2, picked, landed, gath, lagged, part, going, coming, kept, xgoing, xcoming,
    raw_sem, hist_sem, sib_ss, sib_rs, rs_ss, rs_rs, ag_ss, ag_rs, ring_ss, ring_rs, x_ss, x_rs,
):
    rows = raw_ref.shape[0]
    samples = raw_ref.shape[1]
    win_raw = TD * DECIM
    seg_cols = NWIN * TD
    per_stage = VS // (2 * ZN)
    per_dest = per_stage // 2
    sub_rows = rows // SUBS
    t, g = lax.axis_index("tm"), lax.axis_index("chan")
    tn = lax.axis_size("tm")
    z, xh, c = t // 4, (t // 2) % 2, t % 2
    sibling = (t + 1 - 2 * c, g)
    above = (((z + 1) % ZN) * 4 + xh * 2 + c, g)
    below = (((z + ZN - 1) % ZN) * 4 + xh * 2 + c, g)
    across = (z * 4 + (1 - xh) * 2 + c, g)
    later = ((t + 1) % tn, g)
    earlier = ((t + tn - 1) % tn, g)

    def member(r):
        return (t, (g + r) % GN)

    raw_copies = []
    for w in range(NWIN):
        raw_copies.append(
            pltpu.make_async_copy(
                raw_ref.at[:, pl.ds(w * win_raw, win_raw)],
                raw.at[:, pl.ds(TAPS + w * win_raw, win_raw)],
                raw_sem.at[w],
            )
        )
    for w in reversed(range(NWIN)):
        raw_copies[w].start()

    barrier = pltpu.get_barrier_semaphore()
    peers = [sibling, above, below, across, later, earlier] + [member(r) for r in range(1, GN)]
    for peer in peers:
        pl.semaphore_signal(barrier, inc=1, device_id=peer, device_id_type=MESH)
    pl.semaphore_wait(barrier, len(peers))

    history = pltpu.make_async_remote_copy(
        src_ref=raw_ref.at[:, pl.ds(samples - TAPS, TAPS)],
        dst_ref=raw.at[:, pl.ds(0, TAPS)],
        send_sem=hist_sem.at[0],
        recv_sem=hist_sem.at[1],
        device_id=later,
        device_id_type=MESH,
    )
    history.start()

    def sib_copy(w):
        return pltpu.make_async_remote_copy(
            src_ref=w2.at[:, pl.ds(w * TD, TD)],
            dst_ref=w2.at[:, pl.ds(seg_cols + w * TD, TD)],
            send_sem=sib_ss.at[w],
            recv_sem=sib_rs.at[w],
            device_id=sibling,
            device_id_type=MESH,
        )

    shape = (2 * ZN * per_dest, VS)
    row = lax.broadcasted_iota(jnp.int32, shape, 0)
    lane = lax.broadcasted_iota(jnp.int32, shape, 1)
    stage_of = row // per_stage
    up = (row // per_dest) % 2
    dest = jnp.where(up == 0, z + ZN - 1 - stage_of, z + 1 + stage_of) % ZN
    vrow = ((dest * 2 + up) * 2 + c) * per_dest + row % per_dest
    mine = jnp.where(lane == vrow, src_ref[...].astype(F32), 0.0)
    channel = jnp.sum(mine, axis=1, keepdims=True).astype(jnp.int32) - g * rows
    alive = 1.0 - dead_ref[...].astype(F32)
    here = lax.broadcasted_iota(jnp.int32, (shape[0], rows), 1) == channel
    onehot = jnp.where(here, alive, 0.0).astype(BF16)

    def pick(m):
        picked[m] = jnp.dot(
            onehot, w2[:, m * TD : (m + 1) * TD], preferred_element_type=F32
        ).astype(BF16)

    half_raw = win_raw // 2
    raw_copies[NWIN - 1].wait()
    for w in reversed(range(NWIN)):
        if w > 0:
            raw_copies[w - 1].wait()
        else:
            history.wait()
            raw[:, 0:TAPS] = jnp.where(t > 0, raw[:, 0:TAPS], jnp.zeros((rows, TAPS), BF16))
        dec = []
        for j in range(2):
            first = w * win_raw + j * half_raw
            dec.append(
                lax.dot_general(
                    raw[:, first : first + TAPS + half_raw], fir_ref[...], NT,
                    preferred_element_type=F32,
                ).astype(BF16)
            )
        spectrum = jnp.dot(
            jnp.concatenate(dec, axis=1), table_ref[...], preferred_element_type=F32
        )
        real, imag = spectrum[:, :HALF], spectrum[:, HALF:]
        amplitude = jnp.sqrt(real * real + imag * imag)
        high = amplitude.astype(BF16)
        rest = amplitude - high.astype(F32)
        middle = rest.astype(BF16)
        low = (rest - middle.astype(F32)).astype(BF16)
        level = jnp.dot(high, band_ref[...], preferred_element_type=F32)
        level += jnp.dot(middle, band_ref[...], preferred_element_type=F32)
        level += jnp.dot(low, band_ref[...], preferred_element_type=F32)
        factor = 1.0 / (level / (2 * HW + 1) + 1e-06)
        w2[:, w * TD : w * TD + HALF] = (real * factor).astype(BF16)
        w2[:, w * TD + HALF : (w + 1) * TD] = (imag * factor).astype(BF16)
        sib_copy(w).start()
    for w in reversed(range(NWIN)):
        pick(w)
    for w in reversed(range(NWIN)):
        sib_copy(w).wait_recv()
        pick(NWIN + w)

    def span(s):
        return pl.ds(pl.multiple_of(s * per_stage, per_stage), per_stage)

    def rs_copy(s, r):
        return pltpu.make_async_remote_copy(
            src_ref=picked.at[(g + r) % GN, span(s)],
            dst_ref=landed.at[s, r - 1],
            send_sem=rs_ss.at[s, r - 1],
            recv_sem=rs_rs.at[s, r - 1],
            device_id=member(r),
            device_id_type=MESH,
        )

    def ag_copy(s, r, owner):
        return pltpu.make_async_remote_copy(
            src_ref=gath.at[owner, span(s)],
            dst_ref=gath.at[owner, span(s)],
            send_sem=ag_ss.at[s, r - 1],
            recv_sem=ag_rs.at[s, r - 1],
            device_id=member(r),
            device_id_type=MESH,
        )

    def send_picked(s):
        for r in range(1, GN):
            rs_copy(s, r).start()

    def combine(s):
        for r in range(1, GN):
            rs_copy(s, r).wait_recv()
        total = picked[g, span(s)].astype(F32)
        for r in range(1, GN):
            total += landed[s, r - 1].astype(F32)
        gath[g, span(s)] = total.astype(BF16)
        for r in range(1, GN):
            ag_copy(s, r, g).start()

    def rotate(s):
        cos = [lag_ref[m : m + 1, :HALF] for m in range(5)]
        sin = [lag_ref[m : m + 1, HALF:] for m in range(5)]
        for m in range(GN):
            for h in range(2):
                first = pl.multiple_of(s * per_stage + h * per_dest, per_dest)
                a = gath[m, pl.ds(first, per_dest), :HALF].astype(F32)
                b = gath[m, pl.ds(first, per_dest), HALF:].astype(F32)

                def put(lag, real, imag):
                    at = (h * NLAG + lag) * per_dest
                    lagged[at : at + per_dest, m * TD : m * TD + HALF] = real.astype(BF16)
                    lagged[at : at + per_dest, m * TD + HALF : (m + 1) * TD] = imag.astype(BF16)

                mid = NLAG // 2
                put(mid, a * cos[0], b * cos[0])
                for n in range(1, mid + 1):
                    ac, bs, bc, as_ = a * cos[n], b * sin[n], b * cos[n], a * sin[n]
                    put(mid - n, ac - bs, bc + as_)
                    if n < mid:
                        put(mid + n, ac + bs, bc - as_)

    def ring_copy(s, h, u):
        where = (h, s, pl.ds(u * sub_rows, sub_rows))
        return pltpu.make_async_remote_copy(
            src_ref=going.at[where],
            dst_ref=coming.at[where],
            send_sem=ring_ss.at[h, s, u],
            recv_sem=ring_rs.at[h, s, u],
            device_id=above if h == 0 else below,
            device_id_type=MESH,
        )

    def x_copy(u):
        return pltpu.make_async_remote_copy(
            src_ref=xgoing.at[pl.ds(u * sub_rows, sub_rows)],
            dst_ref=xcoming.at[pl.ds(u * sub_rows, sub_rows)],
            send_sem=x_ss.at[u],
            recv_sem=x_rs.at[u],
            device_id=across,
            device_id_type=MESH,
        )

    lanes = NLAG * per_dest
    for s in range(LEAD_RS):
        send_picked(s)
    for s in range(LEAD_AG):
        combine(s)

    def stage(s, carry):
        @pl.when(s + LEAD_AG < ZN)
        def _():
            combine(s + LEAD_AG)

        @pl.when(s + LEAD_RS < ZN)
        def _():
            send_picked(s + LEAD_RS)

        for r in range(1, GN):
            ag_copy(s, r, (g + GN - r) % GN).wait_recv()
        rotate(s)
        for u in range(SUBS):
            at = slice(u * sub_rows, (u + 1) * sub_rows)
            part[at] = lax.dot_general(
                w2[at], lagged[...], NT, preferred_element_type=F32
            )

            @pl.when(s > 0)
            def _():
                for h in range(2):
                    ring_copy(s - 1, h, u).wait_recv()
                    cols = slice(h * lanes, (h + 1) * lanes)
                    part[at, cols] += coming[h, s - 1, at].astype(F32)

            @pl.when(s < ZN - 1)
            def _():
                for h in range(2):
                    going[h, s, at] = part[at, h * lanes : (h + 1) * lanes].astype(BF16)
                    ring_copy(s, h, u).start()

            @pl.when(s == ZN - 1)
            def _():
                low, high = part[at, :lanes], part[at, lanes:]
                kept[at] = jnp.where(xh == 0, low, high)
                xgoing[at] = jnp.where(xh == 0, high, low).astype(BF16)
                x_copy(u).start()

        return carry

    lax.fori_loop(0, ZN, stage, 0)

    for u in range(SUBS):
        x_copy(u).wait_recv()
    total = (kept[...] + xcoming[...].astype(F32)).T * alive
    for lag in range(NLAG):
        out_ref[:, lag, :] = total[lag * per_dest : (lag + 1) * per_dest]

    for w in range(NWIN):
        sib_copy(w).wait_send()

    def drain(s, carry):
        for r in range(1, GN):
            rs_copy(s, r).wait_send()
            ag_copy(s, r, g).wait_send()
        return carry

    lax.fori_loop(0, ZN, drain, 0)

    def drain_ring(s, carry):
        for h in range(2):
            for u in range(SUBS):
                ring_copy(s, h, u).wait_send()
        return carry

    lax.fori_loop(0, ZN - 1, drain_ring, 0)
    for u in range(SUBS):
        x_copy(u).wait_send()


def local(raw_traces, fir_taps, sources, dead_flags):
    rows, samples = raw_traces.shape
    tn = lax.axis_size("tm")
    gain = 1.0 / math.sqrt(tn * NWIN * TD)
    per_stage = VS // (2 * ZN)
    per_dest = per_stage // 2
    cols = 2 * NWIN * TD
    vmem = pl.BlockSpec(memory_space=pltpu.VMEM)
    dma = pltpu.SemaphoreType.DMA
    return pl.pallas_call(
        kernel,
        name="correlate",
        out_shape=jax.ShapeDtypeStruct((per_dest, NLAG, rows), F32),
        in_specs=[pl.BlockSpec(memory_space=pl.ANY)] + [vmem] * 6,
        out_specs=vmem,
        scratch_shapes=[
            pltpu.VMEM((rows, TAPS + samples), BF16),
            pltpu.VMEM((rows, cols), BF16),
            pltpu.VMEM((GN, VS // 2, TD), BF16),
            pltpu.VMEM((ZN, GN - 1, per_stage, TD), BF16),
            pltpu.VMEM((GN, VS // 2, TD), BF16),
            pltpu.VMEM((2 * NLAG * per_dest, cols), BF16),
            pltpu.VMEM((rows, 2 * NLAG * per_dest), F32),
            pltpu.VMEM((2, ZN - 1, rows, NLAG * per_dest), BF16),
            pltpu.VMEM((2, ZN - 1, rows, NLAG * per_dest), BF16),
            pltpu.VMEM((rows, NLAG * per_dest), F32),
            pltpu.VMEM((rows, NLAG * per_dest), BF16),
            pltpu.VMEM((rows, NLAG * per_dest), BF16),
            dma((NWIN,)),
            dma((2,)),
            dma((NWIN,)),
            dma((NWIN,)),
            dma((ZN, GN - 1)),
            dma((ZN, GN - 1)),
            dma((ZN, GN - 1)),
            dma((ZN, GN - 1)),
            dma((2, ZN - 1, SUBS)),
            dma((2, ZN - 1, SUBS)),
            dma((SUBS,)),
            dma((SUBS,)),
        ],
        compiler_params=pltpu.CompilerParams(
            collective_id=0, has_side_effects=True, vmem_limit_bytes=56 * 1024 * 1024
        ),
    )(
        raw_traces,
        fir_rows(fir_taps, HALF),
        dft_table(),
        band_matrix(),
        lag_tables(gain),
        sources[None, :],
        dead_flags[None, :],
    )


def solution(mesh):
    return jax.shard_map(
        local,
        mesh=mesh,
        in_specs=(P("chan", "tm"), P(), P(), P("chan")),
        out_specs=P("tm", None, "chan"),
        check_vma=False,
    )
```

```python
import functools
import math

import jax
import jax.numpy as jnp
import numpy as np
from jax import lax
from jax.experimental import pallas as pl
from jax.experimental.pallas import tpu as pltpu
from jax.sharding import PartitionSpec as P

VS = 512
TD = 256
NWIN = 4
NLAG = 8
HW = 32
TAPS = 128
DECIM = 4
HALF = TD // 2
MESH = pl.DeviceIdType.MESH
F32 = jnp.float32
BF16 = jnp.bfloat16
NT = (((1,), (1,)), ((), ()))

ZN = 8
GN = 8
SUBS = 2
EARLY = 2
AHEAD = 3
HOPS = 7
VMEM_LIMIT = 63 * 1024 * 1024


def dft_table():
    phase = np.arange(TD)[:, None] * np.arange(HALF)[None, :] % TD
    angles = np.float32(2.0 * math.pi / TD) * phase.astype(np.float32)
    return jnp.asarray(np.concatenate([np.cos(angles), -np.sin(angles)], axis=1), dtype=BF16)


def lag_tables(gain):
    phase = np.arange(NLAG)[:, None] * np.arange(HALF)[None, :] % TD
    angles = np.float32(2.0 * math.pi / TD) * phase.astype(np.float32)
    both = np.concatenate([np.cos(angles), np.sin(angles)], axis=1)
    return jnp.asarray((both * np.float32(gain)).astype(np.float32))


def band_matrix():
    bins = np.arange(HALF)
    near = np.abs(bins[:, None] - bins[None, :]) <= HW
    return jnp.asarray(np.concatenate([near, near], axis=0), dtype=BF16)


def kernel(
    raw_ref, taps_hbm, table_hbm, band_hbm, lag_hbm, src_hbm, dead_hbm, out_ref,
    taps_ref, table_ref, band_ref, lag_ref, src_ref, dead_ref, raw, w2, picked, landed, gath, lagged, part, own_go, own_come, far_go, far_come, x_go, x_come, kept,
    small_sem, raw_sem, hist_sem, sib_ss, sib_rs, rs_ss, rs_rs, ag_ss, ag_rs,
    own_ss, own_rs, far_ss, far_rs, x_ss, x_rs,
):
    rows, samples = raw_ref.shape
    win_raw = TD * DECIM
    seg_cols = NWIN * TD
    per_stage = VS // (2 * ZN)
    per_dest = per_stage // 2
    lanes = NLAG * per_dest
    sub_rows = rows // SUBS
    t, g = lax.axis_index("tm"), lax.axis_index("chan")
    tn = lax.axis_size("tm")
    z, xh, c = t // 4, (t // 2) % 2, t % 2
    own = (xh + c) % 2
    own_z = (z + ZN + 1 - 2 * own) % ZN
    far_z = (z + ZN - 1 + 2 * own) % ZN
    sibling = (t + 1 - 2 * c, g)
    own_next = (own_z * 4 + xh * 2 + c, g)
    far_next = (far_z * 4 + xh * 2 + c, g)
    diagonal = (far_z * 4 + (1 - xh) * 2 + c, g)
    diagonal_from = (own_z * 4 + (1 - xh) * 2 + c, g)
    across = (z * 4 + (1 - xh) * 2 + c, g)
    later = ((t + 1) % tn, g)
    earlier = ((t + tn - 1) % tn, g)

    def member(r):
        return (t, (g + r) % GN)

    barrier = pltpu.get_barrier_semaphore()
    peers = [sibling, own_next, far_next, diagonal, diagonal_from, across, later, earlier]
    peers += [member(r) for r in range(1, GN)]
    for peer in peers:
        pl.semaphore_signal(barrier, inc=1, device_id=peer, device_id_type=MESH)

    raw_copies = [
        pltpu.make_async_copy(
            raw_ref.at[:, pl.ds(w * win_raw, win_raw)],
            raw.at[:, pl.ds(TAPS + w * win_raw, win_raw)],
            raw_sem.at[w],
        )
        for w in range(NWIN)
    ]
    small_copies = [
        pltpu.make_async_copy(here, there, small_sem.at[i])
        for i, (here, there) in enumerate(
            [
                (taps_hbm, taps_ref), (src_hbm, src_ref), (dead_hbm, dead_ref),
                (table_hbm, table_ref), (band_hbm, band_ref), (lag_hbm, lag_ref),
            ]
        )
    ]
    for copy in small_copies:
        copy.start()
    for w in reversed(range(NWIN)):
        raw_copies[w].start()
    for copy in small_copies[:3]:
        copy.wait()

    half_raw = win_raw // 2
    width = TAPS + half_raw
    fir = jnp.concatenate(
        [
            jnp.broadcast_to(taps_ref[...].astype(F32), (HALF, TAPS)),
            jnp.zeros((HALF, half_raw), F32),
        ],
        axis=1,
    )
    fir = pltpu.roll(fir, 1, 1)
    out_row = lax.broadcasted_iota(jnp.int32, (HALF, width), 0)
    for bit in range(7):
        fir = jnp.where((out_row >> bit) % 2 == 1, pltpu.roll(fir, DECIM << bit, 1), fir)
    fir = fir.astype(BF16)

    shape = (2 * ZN * per_dest, VS)
    row = lax.broadcasted_iota(jnp.int32, shape, 0)
    lane = lax.broadcasted_iota(jnp.int32, shape, 1)
    stage_of = row // per_stage
    ring = (row // per_dest) % 2
    dest = jnp.where(ring == 0, z + ZN - 1 - stage_of, z + 1 + stage_of) % ZN
    vrow = ((dest * 2 + (ring + c) % 2) * 2 + c) * per_dest + row % per_dest
    mine = jnp.where(lane == vrow, src_ref[...].astype(F32), 0.0)
    channel = jnp.sum(mine, axis=1, keepdims=True).astype(jnp.int32) - g * rows
    alive = 1.0 - dead_ref[...].astype(F32).reshape(1, rows)
    here = lax.broadcasted_iota(jnp.int32, (shape[0], rows), 1) == channel
    onehot = jnp.where(here, alive, 0.0).astype(BF16)

    def sib_copy(w):
        return pltpu.make_async_remote_copy(
            src_ref=w2.at[:, pl.ds(w * TD, TD)],
            dst_ref=w2.at[:, pl.ds(seg_cols + w * TD, TD)],
            send_sem=sib_ss.at[w],
            recv_sem=sib_rs.at[w],
            device_id=sibling,
            device_id_type=MESH,
        )

    def window(w):
        dec = []
        for j in range(2):
            first = w * win_raw + j * half_raw
            dec.append(
                lax.dot_general(
                    raw[:, first : first + width], fir, NT, preferred_element_type=F32
                ).astype(BF16)
            )
        spectrum = jnp.dot(
            jnp.concatenate(dec, axis=1), table_ref[...], preferred_element_type=F32
        )
        real, imag = spectrum[:, :HALF], spectrum[:, HALF:]
        amplitude = jnp.sqrt(real * real + imag * imag)
        high = amplitude.astype(BF16)
        low = (amplitude - high.astype(F32)).astype(BF16)
        level = jnp.dot(
            jnp.concatenate([high, low], axis=1), band_ref[...], preferred_element_type=F32
        )
        factor = 1.0 / (level * (1.0 / (2 * HW + 1)) + 1e-06)
        w2[:, w * TD : w * TD + HALF] = (real * factor).astype(BF16)
        w2[:, w * TD + HALF : (w + 1) * TD] = (imag * factor).astype(BF16)

    def span(s):
        return pl.ds(pl.multiple_of(s * per_stage, per_stage), per_stage)

    def rs_copy(s, r):
        return pltpu.make_async_remote_copy(
            src_ref=picked.at[(g + r) % GN, span(s)],
            dst_ref=landed.at[s, r - 1],
            send_sem=rs_ss,
            recv_sem=rs_rs.at[s],
            device_id=member(r),
            device_id_type=MESH,
        )

    def ag_copy(s, r):
        return pltpu.make_async_remote_copy(
            src_ref=gath.at[0, span(s)],
            dst_ref=gath.at[r, span(s)],
            send_sem=ag_ss,
            recv_sem=ag_rs.at[s],
            device_id=member(r),
            device_id_type=MESH,
        )

    def pick(m):
        picked[m] = jnp.dot(
            onehot, w2[:, m * TD : (m + 1) * TD], preferred_element_type=F32
        ).astype(BF16)
        r = (m + GN - g) % GN

        @pl.when(r != 0)
        def _():
            for s in range(EARLY):
                rs_copy(s, r).start()

    def send_picked(s):
        for r in range(1, GN):
            rs_copy(s, r).start()

    def combine(s):
        pltpu.make_async_copy(landed.at[s], landed.at[s], rs_rs.at[s]).wait()
        total = picked[g, span(s)].astype(F32)
        for r in range(1, GN):
            total += landed[s, r - 1].astype(F32)
        gath[0, span(s)] = total.astype(BF16)
        for r in range(1, GN):
            ag_copy(s, r).start()

    def ag_wait(s):
        there = gath.at[pl.ds(1, GN - 1), span(s)]
        pltpu.make_async_copy(there, there, ag_rs.at[s]).wait()

    def rotate(s):
        cos = [lag_ref[m : m + 1, :HALF] for m in range(5)]
        sin = [lag_ref[m : m + 1, HALF:] for m in range(5)]
        for r in range(GN):
            col = pl.multiple_of((g + GN - r) % GN * TD, TD)
            for h in range(2):
                first = pl.multiple_of(s * per_stage + h * per_dest, per_dest)
                a = gath[r, pl.ds(first, per_dest), :HALF].astype(F32)
                b = gath[r, pl.ds(first, per_dest), HALF:].astype(F32)

                def put(lag, real, imag):
                    at = (h * NLAG + lag) * per_dest
                    both = jnp.concatenate([real.astype(BF16), imag.astype(BF16)], axis=1)
                    lagged[at : at + per_dest, pl.ds(col, TD)] = both

                mid = NLAG // 2
                put(mid, a * cos[0], b * cos[0])
                for n in range(1, mid + 1):
                    ac, bs, bc, as_ = a * cos[n], b * sin[n], b * cos[n], a * sin[n]
                    put(mid - n, ac - bs, bc + as_)
                    if n < mid:
                        put(mid + n, ac + bs, bc - as_)

    def piece(u):
        return pl.ds(u * sub_rows, sub_rows)

    def own_copy(s, u):
        return pltpu.make_async_remote_copy(
            src_ref=own_go.at[s, piece(u)],
            dst_ref=own_come.at[s, piece(u)],
            send_sem=own_ss,
            recv_sem=own_rs.at[s, u],
            device_id=own_next,
            device_id_type=MESH,
        )

    def far_copy(s, u, to):
        return pltpu.make_async_remote_copy(
            src_ref=far_go.at[s, piece(u)],
            dst_ref=far_come.at[s, piece(u)],
            send_sem=far_ss,
            recv_sem=far_rs.at[s, u],
            device_id=to,
            device_id_type=MESH,
        )

    def x_copy(s, u):
        return pltpu.make_async_remote_copy(
            src_ref=x_go.at[s - HOPS, piece(u)],
            dst_ref=x_come.at[s - HOPS, piece(u)],
            send_sem=x_ss,
            recv_sem=x_rs.at[s - HOPS, u],
            device_id=across,
            device_id_type=MESH,
        )

    own_lanes = pl.ds(pl.multiple_of(own * lanes, lanes), lanes)
    far_lanes = pl.ds(pl.multiple_of((1 - own) * lanes, lanes), lanes)

    def dot(s, u):
        at = slice(u * sub_rows, (u + 1) * sub_rows)
        part[s % 2, at] = lax.dot_general(w2[at], lagged[...], NT, preferred_element_type=F32)

        @pl.when(s >= HOPS)
        def _():
            x_go[s - HOPS, at] = part[s % 2, at, far_lanes].astype(BF16)
            x_copy(s, u).start()

    def turn(s, u):
        at = slice(u * sub_rows, (u + 1) * sub_rows)

        @pl.when(s > 0)
        def _():
            own_copy(s - 1, u).wait_recv()
            part[s % 2, at, own_lanes] += own_come[s - 1, at].astype(F32)

        @pl.when(s == HOPS)
        def _():
            far_copy(HOPS - 1, u, diagonal).wait_recv()
            part[s % 2, at, own_lanes] += far_come[HOPS - 1, at].astype(F32)

        @pl.when(s >= HOPS)
        def _():
            x_copy(s, u).wait_recv()
            part[s % 2, at, own_lanes] += x_come[s - HOPS, at].astype(F32)

        @pl.when(s < ZN - 1)
        def _():
            own_go[s, at] = part[s % 2, at, own_lanes].astype(BF16)
            own_copy(s, u).start()

        @pl.when(s == ZN - 1)
        def _():
            kept[at] = part[s % 2, at, own_lanes]

        @pl.when((s > 0) & (s < HOPS))
        def _():
            far_copy(s - 1, u, far_next).wait_recv()
            part[s % 2, at, far_lanes] += far_come[s - 1, at].astype(F32)

        @pl.when(s < HOPS)
        def _():
            far_go[s, at] = part[s % 2, at, far_lanes].astype(BF16)

        @pl.when(s < HOPS - 1)
        def _():
            far_copy(s, u, far_next).start()

        @pl.when(s == HOPS - 1)
        def _():
            far_copy(s, u, diagonal).start()

    pl.semaphore_wait(barrier, len(peers))
    history = pltpu.make_async_remote_copy(
        src_ref=raw_ref.at[:, pl.ds(samples - TAPS, TAPS)],
        dst_ref=raw.at[:, pl.ds(0, TAPS)],
        send_sem=hist_sem.at[0],
        recv_sem=hist_sem.at[1],
        device_id=later,
        device_id_type=MESH,
    )
    history.start()
    for copy in small_copies[3:]:
        copy.wait()
    for w in (3, 2):
        raw_copies[w].wait()
    window(3)
    sib_copy(3).start()
    for w in (2, 1):
        raw_copies[w - 1].wait()
        window(w)
        sib_copy(w).start()
    for w in (3, 2, 1):
        pick(w)
    for w in (3, 2):
        sib_copy(w).wait_recv()
        pick(NWIN + w)
    history.wait()
    raw[:, 0:TAPS] = jnp.where(t > 0, raw[:, 0:TAPS], jnp.zeros((rows, TAPS), BF16))
    window(0)
    sib_copy(0).start()
    pick(0)
    sib_copy(1).wait_recv()
    pick(NWIN + 1)
    sib_copy(0).wait_recv()
    pick(NWIN)
    combine(0)
    send_picked(2)
    combine(1)
    send_picked(3)
    combine(2)
    first = jnp.int32(0)
    ag_wait(0)
    rotate(0)
    for u in range(SUBS):
        dot(first, u)
        turn(first, u)
    send_picked(4)
    combine(3)
    ag_wait(1)
    rotate(1)
    for u in range(SUBS):
        dot(first + 1, u)
    send_picked(5)

    def stage(s, carry):
        for u in range(SUBS):
            @pl.when((s >= AHEAD) & (s + 1 < ZN))
            def _():
                if u == 0:
                    ag_wait(s + 1)
                    rotate(s + 1)
                dot(s + 1, u)

            turn(s, u)
            if u == 0:
                @pl.when(s + 3 < ZN)
                def _():
                    combine(s + 3)

                @pl.when(s + 5 < ZN)
                def _():
                    send_picked(s + 5)

        @pl.when(s < AHEAD)
        def _():
            ag_wait(s + 1)
            rotate(s + 1)
            for u in range(SUBS):
                dot(s + 1, u)

        return carry

    lax.fori_loop(1, ZN, stage, 0)

    total = kept[...].T * alive
    for lag in range(NLAG):
        out_ref[:, lag, :] = total[lag * per_dest : (lag + 1) * per_dest]

    for w in range(NWIN):
        sib_copy(w).wait_send()
    sent = [
        (picked.at[pl.ds(0, GN - 1)], rs_ss), (gath.at[pl.ds(0, GN - 1)], ag_ss),
        (own_go, own_ss), (far_go, far_ss), (x_go, x_ss),
    ]
    for what, sem in sent:
        pltpu.make_async_copy(what, what, sem).wait()


def local(raw_traces, fir_taps, sources, dead_flags):
    rows, samples = raw_traces.shape
    tn = lax.axis_size("tm")
    gain = 1.0 / math.sqrt(tn * NWIN * TD)
    per_stage = VS // (2 * ZN)
    per_dest = per_stage // 2
    lanes = NLAG * per_dest
    cols = 2 * NWIN * TD
    hbm = pl.BlockSpec(memory_space=pltpu.HBM)
    vmem = pl.BlockSpec(memory_space=pltpu.VMEM)
    dma = pltpu.SemaphoreType.DMA
    return pl.pallas_call(
        kernel,
        name="correlate",
        out_shape=jax.ShapeDtypeStruct((per_dest, NLAG, rows), F32),
        in_specs=[hbm] * 7,
        out_specs=vmem,
        scratch_shapes=[
            pltpu.VMEM((1, TAPS), BF16),
            pltpu.VMEM((TD, TD), BF16),
            pltpu.VMEM((TD, HALF), BF16),
            pltpu.VMEM((NLAG, TD), F32),
            pltpu.VMEM((1, VS), jnp.int32),
            pltpu.VMEM((rows,), jnp.int32),
            pltpu.VMEM((rows, TAPS + samples), BF16),
            pltpu.VMEM((rows, cols), BF16),
            pltpu.VMEM((GN, VS // 2, TD), BF16),
            pltpu.VMEM((ZN, GN - 1, per_stage, TD), BF16),
            pltpu.VMEM((GN, VS // 2, TD), BF16),
            pltpu.VMEM((2 * lanes, cols), BF16),
            pltpu.VMEM((2, rows, 2 * lanes), F32),
            pltpu.VMEM((ZN - 1, rows, lanes), BF16),
            pltpu.VMEM((ZN - 1, rows, lanes), BF16),
            pltpu.VMEM((HOPS, rows, lanes), BF16),
            pltpu.VMEM((HOPS, rows, lanes), BF16),
            pltpu.VMEM((ZN - HOPS, rows, lanes), BF16),
            pltpu.VMEM((ZN - HOPS, rows, lanes), BF16),
            pltpu.VMEM((rows, lanes), F32),
            dma((6,)),
            dma((NWIN,)),
            dma((2,)),
            dma((NWIN,)),
            dma((NWIN,)),
            dma,
            dma((ZN,)),
            dma,
            dma((ZN,)),
            dma,
            dma((ZN - 1, SUBS)),
            dma,
            dma((HOPS, SUBS)),
            dma,
            dma((ZN - HOPS, SUBS)),
        ],
        compiler_params=pltpu.CompilerParams(
            collective_id=0, has_side_effects=True, vmem_limit_bytes=VMEM_LIMIT
        ),
    )(
        raw_traces,
        fir_taps[None, :],
        dft_table(),
        band_matrix(),
        lag_tables(gain),
        sources[None, :],
        dead_flags,
    )


def solution(mesh):
    return jax.shard_map(
        local,
        mesh=mesh,
        in_specs=(P("chan", "tm"), P(), P(), P("chan")),
        out_specs=P("tm", None, "chan"),
        check_vma=False,
    )
```

```python
import functools
import math

import jax
import jax.numpy as jnp
import numpy as np
from jax import lax
from jax.experimental import pallas as pl
from jax.experimental.pallas import tpu as pltpu
from jax.sharding import PartitionSpec as P

VS = 512
TD = 256
NWIN = 4
NLAG = 8
HW = 32
TAPS = 128
DECIM = 4
HALF = TD // 2
MESH = pl.DeviceIdType.MESH
F32 = jnp.float32
BF16 = jnp.bfloat16
NT = (((1,), (1,)), ((), ()))

ZN = 8
GN = 8
SUBS = 4
DOTS = 2
PAIRS = ((0, 3), (4, 7), (1, 2), (5, 6))
OWNERS = ((0, 5), (2, 7), (1, 4), (3, 6))
LEAD = 2
MOST = 128
AHEAD = 3
HOPS = 7
VMEM_LIMIT = 63 * 1024 * 1024


def dft_table():
    phase = np.arange(TD)[:, None] * np.arange(HALF)[None, :] % TD
    angles = np.float32(2.0 * math.pi / TD) * phase.astype(np.float32)
    return jnp.asarray(np.concatenate([np.cos(angles), -np.sin(angles)], axis=1), dtype=BF16)


def lag_tables(gain):
    phase = np.arange(NLAG)[:, None] * np.arange(HALF)[None, :] % TD
    angles = np.float32(2.0 * math.pi / TD) * phase.astype(np.float32)
    both = np.concatenate([np.cos(angles), np.sin(angles)], axis=1)
    return jnp.asarray((both * np.float32(gain)).astype(np.float32))


def band_matrix():
    bins = np.arange(HALF)
    near = np.abs(bins[:, None] - bins[None, :]) <= HW
    return jnp.asarray(np.concatenate([near, near], axis=0), dtype=BF16)


def kernel(
    raw_ref, taps_hbm, table_hbm, band_hbm, lag_hbm, src_hbm, dead_hbm, out_ref,
    taps_ref, table_ref, band_ref, lag_ref, src_ref, dead_ref, order_ref, raw, w2, picked, landed, gath, lagged, part, own_go, own_come, far_go, far_come, x_go, x_come, kept,
    small_sem, raw_sem, hist_sem, sib_ss, sib_rs, rs_ss, rs_rs, ag_ss, ag_rs,
    own_ss, own_rs, far_ss, far_rs, x_ss, x_rs,
):
    rows, samples = raw_ref.shape
    win_raw = TD * DECIM
    seg_cols = NWIN * TD
    per_stage = VS // (2 * ZN)
    per_dest = per_stage // 2
    lanes = NLAG * per_dest
    sub_rows = rows // SUBS
    per_dot = SUBS // DOTS
    t, g = lax.axis_index("tm"), lax.axis_index("chan")
    tn = lax.axis_size("tm")
    z, xh, c = t // 4, (t // 2) % 2, t % 2
    own = (xh + c) % 2
    own_z = (z + ZN + 1 - 2 * own) % ZN
    far_z = (z + ZN - 1 + 2 * own) % ZN
    sibling = (t + 1 - 2 * c, g)
    own_next = (own_z * 4 + xh * 2 + c, g)
    far_next = (far_z * 4 + xh * 2 + c, g)
    diagonal = (far_z * 4 + (1 - xh) * 2 + c, g)
    diagonal_from = (own_z * 4 + (1 - xh) * 2 + c, g)
    across = (z * 4 + (1 - xh) * 2 + c, g)
    later = ((t + 1) % tn, g)
    earlier = ((t + tn - 1) % tn, g)

    def member(r):
        return (t, (g + r) % GN)

    barrier = pltpu.get_barrier_semaphore()
    peers = [sibling, own_next, far_next, diagonal, diagonal_from, across, later, earlier]
    peers += [member(r) for r in range(1, GN)]
    for peer in peers:
        pl.semaphore_signal(barrier, inc=1, device_id=peer, device_id_type=MESH)

    raw_copies = [
        pltpu.make_async_copy(
            raw_ref.at[:, pl.ds(w * win_raw, win_raw)],
            raw.at[:, pl.ds(TAPS + w * win_raw, win_raw)],
            raw_sem.at[w],
        )
        for w in range(NWIN)
    ]
    small_copies = [
        pltpu.make_async_copy(here, there, small_sem.at[i])
        for i, (here, there) in enumerate(
            [
                (taps_hbm, taps_ref), (src_hbm, src_ref), (dead_hbm, dead_ref),
                (table_hbm, table_ref), (band_hbm, band_ref), (lag_hbm, lag_ref),
            ]
        )
    ]
    for copy in small_copies:
        copy.start()
    for w in reversed(range(NWIN)):
        raw_copies[w].start()
    for copy in small_copies[:3]:
        copy.wait()

    half_raw = win_raw // 2
    width = TAPS + half_raw
    fir = jnp.concatenate(
        [
            jnp.broadcast_to(taps_ref[...].astype(F32), (HALF, TAPS)),
            jnp.zeros((HALF, half_raw), F32),
        ],
        axis=1,
    )
    fir = pltpu.roll(fir, 1, 1)
    out_row = lax.broadcasted_iota(jnp.int32, (HALF, width), 0)
    for bit in range(7):
        fir = jnp.where((out_row >> bit) % 2 == 1, pltpu.roll(fir, DECIM << bit, 1), fir)
    fir = fir.astype(BF16)

    many = 2 * ZN * per_dest
    row = lax.broadcasted_iota(jnp.int32, (many, VS), 0)
    lane = lax.broadcasted_iota(jnp.int32, (many, VS), 1)
    stage_of = row // per_stage
    ring = (row // per_dest) % 2
    dest = jnp.where(ring == 0, z + ZN - 1 - stage_of, z + 1 + stage_of) % ZN
    vrow = ((dest * 2 + (ring + c) % 2) * 2 + c) * per_dest + row % per_dest
    mine = jnp.where(lane == vrow, src_ref[...].astype(F32), 0.0)
    src_col = jnp.sum(mine, axis=1, keepdims=True)
    row, lane = row[:, :many], lane[:, :many]
    src_row = jnp.sum(jnp.where(row == lane, src_col, 0.0), axis=0, keepdims=True)
    group_col = jnp.floor((src_col + 0.5) * (1.0 / rows))
    group_row = jnp.floor((src_row + 0.5) * (1.0 / rows))
    same = jnp.where(group_col == group_row, 1.0, 0.0)
    rank_col = jnp.sum(jnp.where(lane < row, same, 0.0), axis=1, keepdims=True)
    rank_row = jnp.sum(jnp.where(row < lane, same, 0.0), axis=0, keepdims=True)
    me = g.astype(F32)
    slot = lax.broadcasted_iota(jnp.int32, (MOST, many), 0).astype(F32)
    filled = (slot == rank_row) & (group_row == me)
    channel = jnp.sum(jnp.where(filled, src_row - me * rows + 1.0, 0.0), axis=1, keepdims=True)
    alive = 1.0 - dead_ref[...].astype(F32).reshape(1, rows)
    here = lax.broadcasted_iota(jnp.int32, (MOST, rows), 1) + 1 == channel.astype(jnp.int32)
    onehot = jnp.where(here, alive, 0.0).astype(BF16)
    back = jnp.where(group_col > me, me - group_col + GN, me - group_col)
    place = (back * MOST + rank_col).astype(jnp.int32)
    order_ref[...] = jnp.where(
        lax.broadcasted_iota(jnp.int32, (many, GN * MOST), 1) == place, 1.0, 0.0
    ).astype(BF16)

    def sib_copy(w):
        return pltpu.make_async_remote_copy(
            src_ref=w2.at[:, pl.ds(w * TD, TD)],
            dst_ref=w2.at[:, pl.ds(seg_cols + w * TD, TD)],
            send_sem=sib_ss.at[w],
            recv_sem=sib_rs.at[w],
            device_id=sibling,
            device_id_type=MESH,
        )

    def window(w):
        dec = []
        for j in range(2):
            first = w * win_raw + j * half_raw
            dec.append(
                lax.dot_general(
                    raw[:, first : first + width], fir, NT, preferred_element_type=F32
                ).astype(BF16)
            )
        spectrum = jnp.dot(
            jnp.concatenate(dec, axis=1), table_ref[...], preferred_element_type=F32
        )
        real, imag = spectrum[:, :HALF], spectrum[:, HALF:]
        amplitude = jnp.sqrt(real * real + imag * imag)
        high = amplitude.astype(BF16)
        low = (amplitude - high.astype(F32)).astype(BF16)
        level = jnp.dot(
            jnp.concatenate([high, low], axis=1), band_ref[...], preferred_element_type=F32
        )
        factor = 1.0 / (level * (1.0 / (2 * HW + 1)) + 1e-06)
        w2[:, w * TD : w * TD + HALF] = (real * factor).astype(BF16)
        w2[:, w * TD + HALF : (w + 1) * TD] = (imag * factor).astype(BF16)

    def span(s):
        return pl.ds(pl.multiple_of(s * per_stage, per_stage), per_stage)

    def rs_copy(m, p, where, owner, r):
        return pltpu.make_async_remote_copy(
            src_ref=picked.at[m, p],
            dst_ref=landed.at[r, :, pl.ds(where * HALF, HALF)],
            send_sem=rs_ss,
            recv_sem=rs_rs,
            device_id=(t, owner),
            device_id_type=MESH,
        )

    def ag_copy(s, r):
        return pltpu.make_async_remote_copy(
            src_ref=gath.at[0, span(s)],
            dst_ref=gath.at[r, span(s)],
            send_sem=ag_ss.at[s],
            recv_sem=ag_rs.at[s],
            device_id=member(r),
            device_id_type=MESH,
        )

    def pick(m):
        value = jnp.dot(
            onehot, w2[:, m * TD : (m + 1) * TD], preferred_element_type=F32
        ).astype(BF16)
        q = [m in pair for pair in PAIRS].index(True)
        where = PAIRS[q].index(m)
        for p in range(2):
            half = value[:, p * HALF : (p + 1) * HALF]
            picked[m, p] = half
            r = (OWNERS[q][p] + GN - g) % GN

            @pl.when(r != 0)
            def _():
                rs_copy(m, p, where, OWNERS[q][p], r).start()

            @pl.when(r == 0)
            def _():
                landed[0, :, where * HALF : (where + 1) * HALF] = half

    def combine():
        there = landed.at[pl.ds(1, GN - 1)]
        pltpu.make_async_copy(there, there, rs_rs).wait()
        gath[0] = jnp.dot(
            order_ref[...], landed[...].reshape(GN * MOST, TD), preferred_element_type=F32
        ).astype(BF16)

    def share(s):
        for r in range(1, GN):
            ag_copy(s, r).start()

    def shared(s):
        sent = gath.at[pl.ds(0, GN - 1), span(s)]
        pltpu.make_async_copy(sent, sent, ag_ss.at[s]).wait()

    def ag_wait(s):
        there = gath.at[pl.ds(1, GN - 1), span(s)]
        pltpu.make_async_copy(there, there, ag_rs.at[s]).wait()

    def rotate(s):
        cos = [lag_ref[m : m + 1, :HALF] for m in range(5)]
        sin = [lag_ref[m : m + 1, HALF:] for m in range(5)]
        for m in range(GN):
            q = [m in pair for pair in PAIRS].index(True)
            off = PAIRS[q].index(m) * HALF
            re_at, im_at = [(g + GN - owner) % GN for owner in OWNERS[q]]
            for h in range(2):
                first = pl.multiple_of(s * per_stage + h * per_dest, per_dest)
                a = gath[re_at, pl.ds(first, per_dest), off : off + HALF].astype(F32)
                b = gath[im_at, pl.ds(first, per_dest), off : off + HALF].astype(F32)

                def put(lag, real, imag):
                    at = (h * NLAG + lag) * per_dest
                    both = jnp.concatenate([real.astype(BF16), imag.astype(BF16)], axis=1)
                    lagged[at : at + per_dest, m * TD : (m + 1) * TD] = both

                mid = NLAG // 2
                put(mid, a * cos[0], b * cos[0])
                for n in range(1, mid + 1):
                    ac, bs, bc, as_ = a * cos[n], b * sin[n], b * cos[n], a * sin[n]
                    put(mid - n, ac - bs, bc + as_)
                    if n < mid:
                        put(mid + n, ac + bs, bc - as_)

    def piece(u):
        return pl.ds(u * sub_rows, sub_rows)

    def own_copy(s, u):
        return pltpu.make_async_remote_copy(
            src_ref=own_go.at[s, piece(u)],
            dst_ref=own_come.at[s, piece(u)],
            send_sem=own_ss,
            recv_sem=own_rs.at[s, u],
            device_id=own_next,
            device_id_type=MESH,
        )

    def far_copy(s, u, to):
        return pltpu.make_async_remote_copy(
            src_ref=far_go.at[s, piece(u)],
            dst_ref=far_come.at[s, piece(u)],
            send_sem=far_ss,
            recv_sem=far_rs.at[s, u],
            device_id=to,
            device_id_type=MESH,
        )

    def x_copy(s, u):
        return pltpu.make_async_remote_copy(
            src_ref=x_go.at[s - HOPS, piece(u)],
            dst_ref=x_come.at[s - HOPS, piece(u)],
            send_sem=x_ss,
            recv_sem=x_rs.at[s - HOPS, u],
            device_id=across,
            device_id_type=MESH,
        )

    own_lanes = pl.ds(pl.multiple_of(own * lanes, lanes), lanes)
    far_lanes = pl.ds(pl.multiple_of((1 - own) * lanes, lanes), lanes)

    def dot(s, d):
        at = slice(d * per_dot * sub_rows, (d + 1) * per_dot * sub_rows)
        part[s % 2, at] = lax.dot_general(w2[at], lagged[...], NT, preferred_element_type=F32)

        @pl.when(s >= HOPS)
        def _():
            x_go[s - HOPS, at] = part[s % 2, at, far_lanes].astype(BF16)
            for u in range(d * per_dot, (d + 1) * per_dot):
                x_copy(s, u).start()

    def turn(s, u):
        at = slice(u * sub_rows, (u + 1) * sub_rows)

        @pl.when(s > 0)
        def _():
            own_copy(s - 1, u).wait_recv()
            part[s % 2, at, own_lanes] += own_come[s - 1, at].astype(F32)

        @pl.when(s == HOPS)
        def _():
            far_copy(HOPS - 1, u, diagonal).wait_recv()
            part[s % 2, at, own_lanes] += far_come[HOPS - 1, at].astype(F32)

        @pl.when(s >= HOPS)
        def _():
            x_copy(s, u).wait_recv()
            part[s % 2, at, own_lanes] += x_come[s - HOPS, at].astype(F32)

        @pl.when(s < ZN - 1)
        def _():
            own_go[s, at] = part[s % 2, at, own_lanes].astype(BF16)
            own_copy(s, u).start()

        @pl.when(s == ZN - 1)
        def _():
            kept[at] = part[s % 2, at, own_lanes]

        @pl.when((s > 0) & (s < HOPS))
        def _():
            far_copy(s - 1, u, far_next).wait_recv()
            part[s % 2, at, far_lanes] += far_come[s - 1, at].astype(F32)

        @pl.when(s < HOPS)
        def _():
            far_go[s, at] = part[s % 2, at, far_lanes].astype(BF16)

        @pl.when(s < HOPS - 1)
        def _():
            far_copy(s, u, far_next).start()

        @pl.when(s == HOPS - 1)
        def _():
            far_copy(s, u, diagonal).start()

    pl.semaphore_wait(barrier, len(peers))
    history = pltpu.make_async_remote_copy(
        src_ref=raw_ref.at[:, pl.ds(samples - TAPS, TAPS)],
        dst_ref=raw.at[:, pl.ds(0, TAPS)],
        send_sem=hist_sem.at[0],
        recv_sem=hist_sem.at[1],
        device_id=later,
        device_id_type=MESH,
    )
    history.start()
    for copy in small_copies[3:]:
        copy.wait()
    for w in (3, 2):
        raw_copies[w].wait()
    window(3)
    sib_copy(3).start()
    for w in (2, 1):
        raw_copies[w - 1].wait()
        window(w)
        sib_copy(w).start()
    for w in (3, 2, 1):
        pick(w)
    for w in (3, 2):
        sib_copy(w).wait_recv()
        pick(NWIN + w)
    history.wait()
    raw[:, 0:TAPS] = jnp.where(t > 0, raw[:, 0:TAPS], jnp.zeros((rows, TAPS), BF16))
    window(0)
    sib_copy(0).start()
    pick(0)
    sib_copy(1).wait_recv()
    pick(NWIN + 1)
    sib_copy(0).wait_recv()
    pick(NWIN)
    combine()
    for s in range(LEAD):
        share(s)
        shared(s)
    share(LEAD)
    first = jnp.int32(0)
    ag_wait(0)
    rotate(0)
    for d in range(DOTS):
        dot(first, d)
        for u in range(d * per_dot, (d + 1) * per_dot):
            turn(first, u)
    shared(LEAD)
    share(LEAD + 1)
    ag_wait(1)
    rotate(1)
    for d in range(DOTS):
        dot(first + 1, d)

    def stage(s, carry):
        @pl.when(s + LEAD < ZN)
        def _():
            shared(s + LEAD)

        @pl.when(s + LEAD + 1 < ZN)
        def _():
            share(s + LEAD + 1)

        for d in range(DOTS):
            @pl.when((s >= AHEAD) & (s + 1 < ZN))
            def _():
                if d == 0:
                    ag_wait(s + 1)
                    rotate(s + 1)
                dot(s + 1, d)

            for u in range(d * per_dot, (d + 1) * per_dot):
                turn(s, u)

        @pl.when(s < AHEAD)
        def _():
            ag_wait(s + 1)
            rotate(s + 1)
            for d in range(DOTS):
                dot(s + 1, d)

        return carry

    lax.fori_loop(1, ZN, stage, 0)

    total = kept[...].T * alive
    for lag in range(NLAG):
        out_ref[:, lag, :] = total[lag * per_dest : (lag + 1) * per_dest]

    for w in range(NWIN):
        sib_copy(w).wait_send()
    sent = [
        (landed.at[pl.ds(1, GN - 1)], rs_ss),
        (own_go, own_ss), (far_go, far_ss), (x_go, x_ss),
    ]
    for what, sem in sent:
        pltpu.make_async_copy(what, what, sem).wait()


def local(raw_traces, fir_taps, sources, dead_flags):
    rows, samples = raw_traces.shape
    tn = lax.axis_size("tm")
    gain = 1.0 / math.sqrt(tn * NWIN * TD)
    per_stage = VS // (2 * ZN)
    per_dest = per_stage // 2
    lanes = NLAG * per_dest
    cols = 2 * NWIN * TD
    hbm = pl.BlockSpec(memory_space=pltpu.HBM)
    vmem = pl.BlockSpec(memory_space=pltpu.VMEM)
    dma = pltpu.SemaphoreType.DMA
    return pl.pallas_call(
        kernel,
        name="correlate",
        out_shape=jax.ShapeDtypeStruct((per_dest, NLAG, rows), F32),
        in_specs=[hbm] * 7,
        out_specs=vmem,
        scratch_shapes=[
            pltpu.VMEM((1, TAPS), BF16),
            pltpu.VMEM((TD, TD), BF16),
            pltpu.VMEM((TD, HALF), BF16),
            pltpu.VMEM((NLAG, TD), F32),
            pltpu.VMEM((1, VS), jnp.int32),
            pltpu.VMEM((rows,), jnp.int32),
            pltpu.VMEM((VS // 2, GN * MOST), BF16),
            pltpu.VMEM((rows, TAPS + samples), BF16),
            pltpu.VMEM((rows, cols), BF16),
            pltpu.VMEM((GN, 2, MOST, HALF), BF16),
            pltpu.VMEM((GN, MOST, TD), BF16),
            pltpu.VMEM((GN, VS // 2, TD), BF16),
            pltpu.VMEM((2 * lanes, cols), BF16),
            pltpu.VMEM((2, rows, 2 * lanes), F32),
            pltpu.VMEM((ZN - 1, rows, lanes), BF16),
            pltpu.VMEM((ZN - 1, rows, lanes), BF16),
            pltpu.VMEM((HOPS, rows, lanes), BF16),
            pltpu.VMEM((HOPS, rows, lanes), BF16),
            pltpu.VMEM((ZN - HOPS, rows, lanes), BF16),
            pltpu.VMEM((ZN - HOPS, rows, lanes), BF16),
            pltpu.VMEM((rows, lanes), F32),
            dma((6,)),
            dma((NWIN,)),
            dma((2,)),
            dma((NWIN,)),
            dma((NWIN,)),
            dma,
            dma,
            dma((ZN,)),
            dma((ZN,)),
            dma,
            dma((ZN - 1, SUBS)),
            dma,
            dma((HOPS, SUBS)),
            dma,
            dma((ZN - HOPS, SUBS)),
        ],
        compiler_params=pltpu.CompilerParams(
            collective_id=0, has_side_effects=True, vmem_limit_bytes=VMEM_LIMIT
        ),
    )(
        raw_traces,
        fir_taps[None, :],
        dft_table(),
        band_matrix(),
        lag_tables(gain),
        sources[None, :],
        dead_flags,
    )


def solution(mesh):
    return jax.shard_map(
        local,
        mesh=mesh,
        in_specs=(P("chan", "tm"), P(), P(), P("chan")),
        out_specs=P("tm", None, "chan"),
        check_vma=False,
    )
```

```python
import functools
import math

import jax
import jax.numpy as jnp
import numpy as np
from jax import lax
from jax.experimental import pallas as pl
from jax.experimental.pallas import tpu as pltpu
from jax.sharding import PartitionSpec as P

VS = 512
TD = 256
NWIN = 4
NLAG = 8
HW = 32
TAPS = 128
DECIM = 4
HALF = TD // 2
MESH = pl.DeviceIdType.MESH
F32 = jnp.float32
BF16 = jnp.bfloat16
NT = (((1,), (1,)), ((), ()))

ZN = 8
GN = 8
SUBS = 4
DOTS = 2
PAIRS = ((0, 3), (4, 7), (1, 2), (5, 6))
OWNERS = ((0, 5), (2, 7), (1, 4), (3, 6))
LEAD = 2
MOST = 128
HOPS = 7
VMEM_LIMIT = 63 * 1024 * 1024


def dft_table():
    phase = np.arange(TD)[:, None] * np.arange(HALF)[None, :] % TD
    angles = np.float32(2.0 * math.pi / TD) * phase.astype(np.float32)
    return jnp.asarray(np.concatenate([np.cos(angles), -np.sin(angles)], axis=1), dtype=BF16)


def lag_tables(gain):
    phase = np.arange(NLAG)[:, None] * np.arange(HALF)[None, :] % TD
    angles = np.float32(2.0 * math.pi / TD) * phase.astype(np.float32)
    both = np.concatenate([np.cos(angles), np.sin(angles)], axis=1)
    return jnp.asarray((both * np.float32(gain)).astype(np.float32))


def band_matrix():
    bins = np.arange(HALF)
    near = np.abs(bins[:, None] - bins[None, :]) <= HW
    return jnp.asarray(np.concatenate([near, near], axis=0), dtype=BF16)


def kernel(
    raw_ref, taps_hbm, table_hbm, band_hbm, lag_hbm, src_hbm, dead_hbm, out_ref,
    taps_ref, table_ref, band_ref, lag_ref, src_ref, dead_ref, order_ref, raw, w2, picked, landed, gath, lagged, part, own_go, own_come, far_go, far_come, x_go, x_come, kept,
    small_sem, raw_sem, hist_sem, sib_ss, sib_rs, rs_ss, rs_rs, ag_ss, ag_rs,
    own_ss, own_rs, far_ss, far_rs, x_ss, x_rs,
):
    rows, samples = raw_ref.shape
    win_raw = TD * DECIM
    seg_cols = NWIN * TD
    per_stage = VS // (2 * ZN)
    per_dest = per_stage // 2
    lanes = NLAG * per_dest
    sub_rows = rows // SUBS
    per_dot = SUBS // DOTS
    t, g = lax.axis_index("tm"), lax.axis_index("chan")
    tn = lax.axis_size("tm")
    z, xh, c = t // 4, (t // 2) % 2, t % 2
    own = (xh + c) % 2
    own_z = (z + ZN + 1 - 2 * own) % ZN
    far_z = (z + ZN - 1 + 2 * own) % ZN
    sibling = (t + 1 - 2 * c, g)
    own_next = (own_z * 4 + xh * 2 + c, g)
    far_next = (far_z * 4 + xh * 2 + c, g)
    diagonal = (far_z * 4 + (1 - xh) * 2 + c, g)
    diagonal_from = (own_z * 4 + (1 - xh) * 2 + c, g)
    across = (z * 4 + (1 - xh) * 2 + c, g)
    later = ((t + 1) % tn, g)
    earlier = ((t + tn - 1) % tn, g)

    def member(r):
        return (t, (g + r) % GN)

    barrier = pltpu.get_barrier_semaphore()
    peers = [sibling, own_next, far_next, diagonal, diagonal_from, across, later, earlier]
    peers += [member(r) for r in range(1, GN)]
    for peer in peers:
        pl.semaphore_signal(barrier, inc=1, device_id=peer, device_id_type=MESH)

    raw_copies = [
        pltpu.make_async_copy(
            raw_ref.at[:, pl.ds(w * win_raw, win_raw)],
            raw.at[:, pl.ds(TAPS + w * win_raw, win_raw)],
            raw_sem.at[w],
        )
        for w in range(NWIN)
    ]
    small_copies = [
        pltpu.make_async_copy(here, there, small_sem.at[i])
        for i, (here, there) in enumerate(
            [
                (taps_hbm, taps_ref), (src_hbm, src_ref), (dead_hbm, dead_ref),
                (table_hbm, table_ref), (band_hbm, band_ref), (lag_hbm, lag_ref),
            ]
        )
    ]
    for copy in small_copies:
        copy.start()
    for w in reversed(range(NWIN)):
        raw_copies[w].start()
    for copy in small_copies[:3]:
        copy.wait()

    half_raw = win_raw // 2
    width = TAPS + half_raw
    fir = jnp.concatenate(
        [
            jnp.broadcast_to(taps_ref[...].astype(F32), (HALF, TAPS)),
            jnp.zeros((HALF, half_raw), F32),
        ],
        axis=1,
    )
    fir = pltpu.roll(fir, 1, 1)
    out_row = lax.broadcasted_iota(jnp.int32, (HALF, width), 0)
    for bit in range(7):
        fir = jnp.where((out_row >> bit) % 2 == 1, pltpu.roll(fir, DECIM << bit, 1), fir)
    fir = fir.astype(BF16)

    many = 2 * ZN * per_dest
    row = lax.broadcasted_iota(jnp.int32, (many, VS), 0)
    lane = lax.broadcasted_iota(jnp.int32, (many, VS), 1)
    stage_of = row // per_stage
    ring = (row // per_dest) % 2
    dest = jnp.where(ring == 0, z + ZN - 1 - stage_of, z + 1 + stage_of) % ZN
    vrow = ((dest * 2 + (ring + c) % 2) * 2 + c) * per_dest + row % per_dest
    mine = jnp.where(lane == vrow, src_ref[...].astype(F32), 0.0)
    src_col = jnp.sum(mine, axis=1, keepdims=True)
    row, lane = row[:, :many], lane[:, :many]
    src_row = jnp.sum(jnp.where(row == lane, src_col, 0.0), axis=0, keepdims=True)
    group_col = jnp.floor((src_col + 0.5) * (1.0 / rows))
    group_row = jnp.floor((src_row + 0.5) * (1.0 / rows))
    same = jnp.where(group_col == group_row, 1.0, 0.0)
    rank_col = jnp.sum(jnp.where(lane < row, same, 0.0), axis=1, keepdims=True)
    rank_row = jnp.sum(jnp.where(row < lane, same, 0.0), axis=0, keepdims=True)
    me = g.astype(F32)
    slot = lax.broadcasted_iota(jnp.int32, (MOST, many), 0).astype(F32)
    filled = (slot == rank_row) & (group_row == me)
    channel = jnp.sum(jnp.where(filled, src_row - me * rows + 1.0, 0.0), axis=1, keepdims=True)
    alive = 1.0 - dead_ref[...].astype(F32).reshape(1, rows)
    here = lax.broadcasted_iota(jnp.int32, (MOST, rows), 1) + 1 == channel.astype(jnp.int32)
    onehot = jnp.where(here, alive, 0.0).astype(BF16)
    def sib_copy(w):
        return pltpu.make_async_remote_copy(
            src_ref=w2.at[:, pl.ds(w * TD, TD)],
            dst_ref=w2.at[:, pl.ds(seg_cols + w * TD, TD)],
            send_sem=sib_ss.at[w],
            recv_sem=sib_rs.at[w],
            device_id=sibling,
            device_id_type=MESH,
        )

    def window(w):
        dec = []
        for j in range(2):
            first = w * win_raw + j * half_raw
            dec.append(
                lax.dot_general(
                    raw[:, first : first + width], fir, NT, preferred_element_type=F32
                ).astype(BF16)
            )
        spectrum = jnp.dot(
            jnp.concatenate(dec, axis=1), table_ref[...], preferred_element_type=F32
        )
        real, imag = spectrum[:, :HALF], spectrum[:, HALF:]
        amplitude = jnp.sqrt(real * real + imag * imag)
        high = amplitude.astype(BF16)
        low = (amplitude - high.astype(F32)).astype(BF16)
        level = jnp.dot(
            jnp.concatenate([high, low], axis=1), band_ref[...], preferred_element_type=F32
        )
        factor = 1.0 / (level * (1.0 / (2 * HW + 1)) + 1e-06)
        w2[:, w * TD : w * TD + HALF] = (real * factor).astype(BF16)
        w2[:, w * TD + HALF : (w + 1) * TD] = (imag * factor).astype(BF16)

    def span(s):
        return pl.ds(pl.multiple_of(s * per_stage, per_stage), per_stage)

    def rs_copy(m, p, where, owner, r):
        return pltpu.make_async_remote_copy(
            src_ref=picked.at[m, p],
            dst_ref=landed.at[r, :, pl.ds(where * HALF, HALF)],
            send_sem=rs_ss,
            recv_sem=rs_rs,
            device_id=(t, owner),
            device_id_type=MESH,
        )

    def ag_copy(s, r):
        return pltpu.make_async_remote_copy(
            src_ref=gath.at[0, span(s)],
            dst_ref=gath.at[r, span(s)],
            send_sem=ag_ss.at[s],
            recv_sem=ag_rs.at[s],
            device_id=member(r),
            device_id_type=MESH,
        )

    def pick(m):
        value = jnp.dot(
            onehot, w2[:, m * TD : (m + 1) * TD], preferred_element_type=F32
        ).astype(BF16)
        q = [m in pair for pair in PAIRS].index(True)
        where = PAIRS[q].index(m)
        for p in range(2):
            half = value[:, p * HALF : (p + 1) * HALF]
            picked[m, p] = half
            r = (OWNERS[q][p] + GN - g) % GN

            @pl.when(r != 0)
            def _():
                rs_copy(m, p, where, OWNERS[q][p], r).start()

            @pl.when(r == 0)
            def _():
                landed[0, :, where * HALF : (where + 1) * HALF] = half

    def combine():
        there = landed.at[pl.ds(1, GN - 1)]
        pltpu.make_async_copy(there, there, rs_rs).wait()
        gath[0] = jnp.dot(
            order_ref[...], landed[...].reshape(GN * MOST, TD), preferred_element_type=F32
        ).astype(BF16)

    def share(s):
        for r in range(1, GN):
            ag_copy(s, r).start()

    def shared(s):
        sent = gath.at[pl.ds(0, GN - 1), span(s)]
        pltpu.make_async_copy(sent, sent, ag_ss.at[s]).wait()

    def ag_wait(s):
        there = gath.at[pl.ds(1, GN - 1), span(s)]
        pltpu.make_async_copy(there, there, ag_rs.at[s]).wait()

    def rotate(s):
        cos = [lag_ref[m : m + 1, :HALF] for m in range(5)]
        sin = [lag_ref[m : m + 1, HALF:] for m in range(5)]
        for m in range(GN):
            q = [m in pair for pair in PAIRS].index(True)
            off = PAIRS[q].index(m) * HALF
            re_at, im_at = [(g + GN - owner) % GN for owner in OWNERS[q]]
            for h in range(2):
                first = pl.multiple_of(s * per_stage + h * per_dest, per_dest)
                a = gath[re_at, pl.ds(first, per_dest), off : off + HALF].astype(F32)
                b = gath[im_at, pl.ds(first, per_dest), off : off + HALF].astype(F32)

                def put(lag, real, imag):
                    at = (h * NLAG + lag) * per_dest
                    both = jnp.concatenate([real.astype(BF16), imag.astype(BF16)], axis=1)
                    lagged[at : at + per_dest, m * TD : (m + 1) * TD] = both

                mid = NLAG // 2
                put(mid, a * cos[0], b * cos[0])
                for n in range(1, mid + 1):
                    ac, bs, bc, as_ = a * cos[n], b * sin[n], b * cos[n], a * sin[n]
                    put(mid - n, ac - bs, bc + as_)
                    if n < mid:
                        put(mid + n, ac + bs, bc - as_)

    def piece(u):
        return pl.ds(u * sub_rows, sub_rows)

    def own_copy(s, u):
        return pltpu.make_async_remote_copy(
            src_ref=own_go.at[s, piece(u)],
            dst_ref=own_come.at[s, piece(u)],
            send_sem=own_ss,
            recv_sem=own_rs.at[s, u],
            device_id=own_next,
            device_id_type=MESH,
        )

    def far_copy(s, u, to):
        return pltpu.make_async_remote_copy(
            src_ref=far_go.at[s, piece(u)],
            dst_ref=far_come.at[s, piece(u)],
            send_sem=far_ss,
            recv_sem=far_rs.at[s, u],
            device_id=to,
            device_id_type=MESH,
        )

    def x_copy(s, u):
        return pltpu.make_async_remote_copy(
            src_ref=x_go.at[s - HOPS, piece(u)],
            dst_ref=x_come.at[s - HOPS, piece(u)],
            send_sem=x_ss,
            recv_sem=x_rs.at[s - HOPS, u],
            device_id=across,
            device_id_type=MESH,
        )

    own_lanes = pl.ds(pl.multiple_of(own * lanes, lanes), lanes)
    far_lanes = pl.ds(pl.multiple_of((1 - own) * lanes, lanes), lanes)

    def dot(s, d):
        at = slice(d * per_dot * sub_rows, (d + 1) * per_dot * sub_rows)
        part[s % 2, at] = lax.dot_general(w2[at], lagged[...], NT, preferred_element_type=F32)

        @pl.when(s >= HOPS)
        def _():
            x_go[s - HOPS, at] = part[s % 2, at, far_lanes].astype(BF16)
            for u in range(d * per_dot, (d + 1) * per_dot):
                x_copy(s, u).start()

    def turn(s, u):
        at = slice(u * sub_rows, (u + 1) * sub_rows)

        @pl.when(s > 0)
        def _():
            own_copy(s - 1, u).wait_recv()
            part[s % 2, at, own_lanes] += own_come[s - 1, at].astype(F32)

        @pl.when(s == HOPS)
        def _():
            far_copy(HOPS - 1, u, diagonal).wait_recv()
            part[s % 2, at, own_lanes] += far_come[HOPS - 1, at].astype(F32)

        @pl.when(s >= HOPS)
        def _():
            x_copy(s, u).wait_recv()
            part[s % 2, at, own_lanes] += x_come[s - HOPS, at].astype(F32)

        @pl.when(s < ZN - 1)
        def _():
            own_go[s, at] = part[s % 2, at, own_lanes].astype(BF16)
            own_copy(s, u).start()

        @pl.when(s == ZN - 1)
        def _():
            kept[at] = part[s % 2, at, own_lanes]

        @pl.when((s > 0) & (s < HOPS))
        def _():
            far_copy(s - 1, u, far_next).wait_recv()
            part[s % 2, at, far_lanes] += far_come[s - 1, at].astype(F32)

        @pl.when(s < HOPS)
        def _():
            far_go[s, at] = part[s % 2, at, far_lanes].astype(BF16)

        @pl.when(s < HOPS - 1)
        def _():
            far_copy(s, u, far_next).start()

        @pl.when(s == HOPS - 1)
        def _():
            far_copy(s, u, diagonal).start()

    pl.semaphore_wait(barrier, len(peers))
    history = pltpu.make_async_remote_copy(
        src_ref=raw_ref.at[:, pl.ds(samples - TAPS, TAPS)],
        dst_ref=raw.at[:, pl.ds(0, TAPS)],
        send_sem=hist_sem.at[0],
        recv_sem=hist_sem.at[1],
        device_id=later,
        device_id_type=MESH,
    )
    history.start()
    for copy in small_copies[3:]:
        copy.wait()
    for w in (3, 2):
        raw_copies[w].wait()
    window(3)
    sib_copy(3).start()
    for w in (2, 1):
        raw_copies[w - 1].wait()
        window(w)
        sib_copy(w).start()
    for w in (3, 2, 1):
        pick(w)
    for w in (3, 2):
        sib_copy(w).wait_recv()
        pick(NWIN + w)
    history.wait()
    raw[:, 0:TAPS] = jnp.where(t > 0, raw[:, 0:TAPS], jnp.zeros((rows, TAPS), BF16))
    window(0)
    sib_copy(0).start()
    pick(0)
    sib_copy(1).wait_recv()
    pick(NWIN + 1)
    sib_copy(0).wait_recv()
    pick(NWIN)
    back = jnp.where(group_col > me, me - group_col + GN, me - group_col)
    place = (back * MOST + rank_col).astype(jnp.int32)
    order_ref[...] = jnp.where(
        lax.broadcasted_iota(jnp.int32, (many, GN * MOST), 1) == place, 1.0, 0.0
    ).astype(BF16)
    combine()
    for s in range(LEAD):
        share(s)
        shared(s)
    share(LEAD)

    def stage(s, carry):
        @pl.when((s >= 0) & (s + LEAD < ZN))
        def _():
            shared(s + LEAD)

        @pl.when((s >= 0) & (s + LEAD + 1 < ZN))
        def _():
            share(s + LEAD + 1)

        for d in range(DOTS):
            @pl.when(s + 1 < ZN)
            def _():
                if d == 0:
                    ag_wait(s + 1)
                    rotate(s + 1)
                dot(s + 1, d)

            @pl.when(s != 0)
            def _():
                for u in range(d * per_dot, (d + 1) * per_dot):
                    turn(jnp.maximum(s, 0), u)

        return carry

    lax.fori_loop(-1, ZN, stage, 0)

    total = kept[...].T * alive
    for lag in range(NLAG):
        out_ref[:, lag, :] = total[lag * per_dest : (lag + 1) * per_dest]

    for w in range(NWIN):
        sib_copy(w).wait_send()
    sent = [
        (landed.at[pl.ds(1, GN - 1)], rs_ss),
        (own_go, own_ss), (far_go, far_ss), (x_go, x_ss),
    ]
    for what, sem in sent:
        pltpu.make_async_copy(what, what, sem).wait()


def local(raw_traces, fir_taps, sources, dead_flags):
    rows, samples = raw_traces.shape
    tn = lax.axis_size("tm")
    gain = 1.0 / math.sqrt(tn * NWIN * TD)
    per_stage = VS // (2 * ZN)
    per_dest = per_stage // 2
    lanes = NLAG * per_dest
    cols = 2 * NWIN * TD
    hbm = pl.BlockSpec(memory_space=pltpu.HBM)
    vmem = pl.BlockSpec(memory_space=pltpu.VMEM)
    dma = pltpu.SemaphoreType.DMA
    return pl.pallas_call(
        kernel,
        name="correlate",
        out_shape=jax.ShapeDtypeStruct((per_dest, NLAG, rows), F32),
        in_specs=[hbm] * 7,
        out_specs=vmem,
        scratch_shapes=[
            pltpu.VMEM((1, TAPS), BF16),
            pltpu.VMEM((TD, TD), BF16),
            pltpu.VMEM((TD, HALF), BF16),
            pltpu.VMEM((NLAG, TD), F32),
            pltpu.VMEM((1, VS), jnp.int32),
            pltpu.VMEM((rows,), jnp.int32),
            pltpu.VMEM((VS // 2, GN * MOST), BF16),
            pltpu.VMEM((rows, TAPS + samples), BF16),
            pltpu.VMEM((rows, cols), BF16),
            pltpu.VMEM((GN, 2, MOST, HALF), BF16),
            pltpu.VMEM((GN, MOST, TD), BF16),
            pltpu.VMEM((GN, VS // 2, TD), BF16),
            pltpu.VMEM((2 * lanes, cols), BF16),
            pltpu.VMEM((2, rows, 2 * lanes), F32),
            pltpu.VMEM((ZN - 1, rows, lanes), BF16),
            pltpu.VMEM((ZN - 1, rows, lanes), BF16),
            pltpu.VMEM((HOPS, rows, lanes), BF16),
            pltpu.VMEM((HOPS, rows, lanes), BF16),
            pltpu.VMEM((ZN - HOPS, rows, lanes), BF16),
            pltpu.VMEM((ZN - HOPS, rows, lanes), BF16),
            pltpu.VMEM((rows, lanes), F32),
            dma((6,)),
            dma((NWIN,)),
            dma((2,)),
            dma((NWIN,)),
            dma((NWIN,)),
            dma,
            dma,
            dma((ZN,)),
            dma((ZN,)),
            dma,
            dma((ZN - 1, SUBS)),
            dma,
            dma((HOPS, SUBS)),
            dma,
            dma((ZN - HOPS, SUBS)),
        ],
        compiler_params=pltpu.CompilerParams(
            collective_id=0, has_side_effects=True, vmem_limit_bytes=VMEM_LIMIT
        ),
    )(
        raw_traces,
        fir_taps[None, :],
        dft_table(),
        band_matrix(),
        lag_tables(gain),
        sources[None, :],
        dead_flags,
    )


def solution(mesh):
    return jax.shard_map(
        local,
        mesh=mesh,
        in_specs=(P("chan", "tm"), P(), P(), P("chan")),
        out_specs=P("tm", None, "chan"),
        check_vma=False,
    )
```
